32 devices in a mesh: row: 8 (over z, y), col: 4 (over x, core).
Axes of the slice: x: 2, y: 2, z: 4, core: 2. Of those that a mesh axis runs over, the one named last changes fastest.
Arguments:
- head_deflections: float32 [256, 3, 2, 1024], P('row', None, None, 'col'), may hold values from -6 to 6
- diag_inverse: float32 [2, 1024, 1024], P(None, None, 'col'), may hold values from -1 to 2, as said below
- coupling: float32 [1024, 1024], P(None, 'col'), may hold values from -0.1875 to 0.1875
- panel_factor: float32 [8192, 2, 1024], P('row', None, 'col'), may hold values from -0.125 to 0.125
- trailing: float32 [256, 3, 8192], P('col', None, 'row'), may hold values from -6 to 6
Outputs:
- solved: float32 [256, 3, 2, 1024], P('row', None, None, 'col')
- rest: float32 [256, 3, 8192], P('col', None, 'row')
The draws below stay inside these ranges and needn't reach their ends.
Inputs may be any that keep to these rules, and one draw needn't show every extreme that they name: Each diag_inverse[p] is lower triangular with a positive diagonal.
All inputs are finite; a program needn't handle non-finite values.
Results may differ from the reference program's by a relative error of at most 0.00007.
Values sent between devices are 32-bit elements; how exact they have to be, the bound alone decides.
No kernel may reach another device: no remote copies, remote signals or barrier semaphores. Data moves between devices by JAX's collectives and lax.ppermute only.
A program may use at most 64 MiB of HBM per device.

```python
import math
import jax
import jax.numpy as jnp
from jax import lax

NB = 1024
STEPS = 256
COMP = 3
TRAIL = 8192


def draw_diag_inverse(key, part):
    key_lower, key_diagonal = jax.random.split(key)
    rows = lax.broadcasted_iota(jnp.int32, (2, NB, NB), 1)
    cols = lax.broadcasted_iota(jnp.int32, (2, NB, NB), 2)
    lower = jax.random.normal(key_lower, (2, NB, NB), jnp.float32)
    lower = lower * (0.6 / math.sqrt(NB))
    diagonal = jnp.exp(jax.random.uniform(key_diagonal, (2, NB, NB), jnp.float32, math.log(0.5), math.log(1.5)))
    return jnp.where(rows > cols, lower, jnp.where(rows == cols, diagonal, 0.0))


def shard_levels(own_key, shape, shards, least, top_value):
    def one(axis_at, blocks):
        draws = jax.random.uniform(jax.random.fold_in(jax.random.fold_in(own_key, 6), axis_at), (blocks,), jnp.float32, least / len(shards), top_value / len(shards))
        return jnp.repeat(jnp.exp(draws), shape[axis_at] // blocks).reshape((-1,) + (1,) * (len(shape) - axis_at - 1))

    loudness = one(*shards[0])
    for cut in shards[1:]:
        loudness = loudness * one(*cut)
    return loudness


def gaussian(stream_key, extent, width, most, pieces=(), kind=jnp.bfloat16):
    drawn = jax.random.normal(stream_key, extent, jnp.float32) * width
    if len(pieces) > 0:
        drawn = shard_levels(stream_key, extent, pieces, -0.22, 0.18) * drawn
    return jnp.clip(drawn, min=-most, max=most).astype(kind)


def setup_inputs(seed: int = 0) -> dict:
    key_list = jax.random.split(jax.random.key(seed), 6)
    head_deflections = gaussian(key_list[0], (STEPS, COMP, 2, NB), 1.0, 6.0, ((0, 8), (3, 4)), jnp.float32)
    diag_inverse = draw_diag_inverse(jax.random.fold_in(key_list[5], 71), 0)
    coupling = gaussian(key_list[2], (NB, NB), NB ** -0.5, 0.1875, ((1, 4),), jnp.float32)
    panel_factor = gaussian(key_list[3], (TRAIL, 2, NB), (2 * NB) ** -0.5, 0.125, ((0, 8), (2, 4)), jnp.float32)
    trailing = gaussian(key_list[4], (STEPS, COMP, TRAIL), 1.0, 6.0, ((0, 4), (2, 8)), jnp.float32)
    return dict(head_deflections=head_deflections, diag_inverse=diag_inverse, coupling=coupling, panel_factor=panel_factor, trailing=trailing)


def reference(head_deflections, diag_inverse, coupling, panel_factor, trailing):
    highest = lax.Precision.HIGHEST
    first_solved = jnp.einsum("ij,skj->ski", diag_inverse[0], head_deflections[:, :, 0, :], precision=highest)
    carried = head_deflections[:, :, 1, :] - jnp.einsum("ij,skj->ski", coupling, first_solved, precision=highest)
    second_solved = jnp.einsum("ij,skj->ski", diag_inverse[1], carried, precision=highest)
    solved = jnp.stack([first_solved, second_solved], axis=2)
    first_update = jnp.einsum("rj,skj->skr", panel_factor[:, 0, :], first_solved, precision=highest)
    second_update = jnp.einsum("rj,skj->skr", panel_factor[:, 1, :], second_solved, precision=highest)
    rest = trailing - first_update - second_update
    return solved, rest
```

```python
import jax
import jax.numpy as jnp
from jax import lax
from jax.sharding import PartitionSpec as P

SOLVE = lax.Precision.HIGHEST
UPDATE = lax.Precision.HIGH


def apply_rows(vectors, matrix, precision):
    return lax.dot_general(
        vectors,
        matrix,
        (((1,), (1,)), ((), ())),
        precision=precision,
        preferred_element_type=jnp.float32,
    )


def apply_pair(vectors, own, other, precision):
    width = own.shape[1]
    near = apply_rows(vectors[:, :width], own, precision)
    return near + apply_rows(vectors[:, width:], other, precision)


def make_body(n_row, n_col):
    n_x = n_col // 2
    n_y = n_x
    n_z = n_row // n_y
    assert n_z == 2 * n_x and n_y * n_z == n_row

    def col_permute(value, pairs):
        return lax.ppermute(value, "col", pairs)

    def core_swap(value):
        return col_permute(value, [(c, c ^ 1) for c in range(n_col)])

    def x_shift(value, step, up_only=False):
        pairs = []
        for x in range(n_x):
            if x + step < n_x or not up_only:
                pairs += [(2 * x + k, 2 * ((x + step) % n_x) + k) for k in range(2)]
        return col_permute(value, pairs)

    def z_round(value, even):
        first, second = even, even ^ 1
        pairs = []
        for z in range(n_z):
            for y in range(n_y):
                for c in range(n_col):
                    x, k = divmod(c, 2)
                    step = first if k == z % 2 else second
                    to = ((z + step) % n_z * n_y + y) * n_col + 2 * x + z % 2
                    pairs.append(((z * n_y + y) * n_col + c, to))
        pairs = [(a, b) for a, b in pairs if a != b]
        return lax.ppermute(value, ("row", "col"), pairs)

    def y_shift(value, step):
        pairs = []
        for z in range(n_z):
            for y in range(n_y):
                pairs.append((z * n_y + y, z * n_y + (y + step) % n_y))
        return lax.ppermute(value, "row", pairs)

    def body(head, diag, coupling, factor, trailing):
        steps, comps, _, quarter = head.shape
        unknowns = diag.shape[1]
        rows = factor.shape[0]
        block = unknowns // n_x
        half = steps // 2
        vecs = half * comps
        col = lax.axis_index("col")
        x, k = col // 2, col % 2
        z = lax.axis_index("row") // n_y
        y = lax.axis_index("row") % n_y
        upper = k == 1

        def turn(value):
            return jnp.where(upper, jnp.roll(value, quarter, axis=-1), value)

        def aim(value):
            return jnp.where(k == z % 2, value, jnp.roll(value, quarter, axis=-1))

        def x_block(value, index):
            return lax.dynamic_slice_in_dim(value, index * block, block, axis=1)

        def x_sum(value, up_only):
            total = x_block(value, x)
            for step in range(1, n_x):
                to = x + step
                to = jnp.minimum(to, n_x - 1) if up_only else to % n_x
                total = total + x_shift(x_block(value, to), step, up_only)
            return total

        split = head.reshape(2, half, comps, 2, quarter).transpose(3, 0, 2, 1, 4)
        split = jnp.where(upper, split[:, ::-1], split)
        split = split.reshape(2, 2 * vecs, quarter)

        coupling_other = core_swap(coupling)
        second_other = core_swap(diag[1])
        factor0, factor1 = factor[:, 0, :], factor[:, 1, :]
        factor0_other = core_swap(factor0)
        factor1_other = core_swap(factor1)

        part = apply_rows(split[0], diag[0], SOLVE)
        part = part[:vecs] + core_swap(part[vecs:])
        first = turn(x_sum(part, True))
        own_rhs = split[1, :vecs]
        rhs = jnp.concatenate([own_rhs, core_swap(split[1, vecs:])], axis=1)

        moved = x_sum(apply_pair(first, coupling, coupling_other, SOLVE), False)
        carried = rhs - turn(moved)
        part = apply_pair(carried, diag[1], second_other, SOLVE)
        second = turn(x_sum(part, True))

        def z_gather(value):
            got = []
            match = k == z % 2
            for even in range(0, n_z, 2):
                one = z_round(value, even)
                two = z_round(value, even + 1)
                if even == 0:
                    one = jnp.where(match, value, one)
                got.append((one, two))
            near = jnp.stack([g[0] for g in got])
            far = jnp.stack([g[1] for g in got])
            return near, far

        zq = (z - jnp.where(k == z % 2, 0, 1)) // 2

        def by_target(stack):
            return [
                lax.dynamic_index_in_dim(stack, (zq - x - t) % n_x, 0, keepdims=False)
                for t in range(n_x)
            ]

        first_near, first_far = z_gather(aim(first))
        second_near, second_far = z_gather(aim(second))

        firsts, seconds = [], []
        for u in range(n_y):
            move = (lambda v, u=u: v) if u == 0 else (lambda v, u=u: y_shift(v, u))
            firsts.append((move(first_near), move(first_far)))
            seconds.append((move(second_near), move(second_far)))

        rest = trailing
        for u in range(n_y):
            for kind in range(2):
                a = by_target(firsts[u][kind])
                b = by_target(seconds[u][kind])
                parts = [
                    apply_pair(p, factor0, factor0_other, UPDATE)
                    + apply_pair(q, factor1, factor1_other, UPDATE)
                    for p, q in zip(a, b)
                ]
                total = parts[0]
                for t in range(1, n_x):
                    total = total + x_shift(parts[t], t)
                total = total.reshape(comps, half, rows).transpose(1, 0, 2)
                at_half = z % 2 if kind == 0 else 1 - z % 2
                at = ((y - u) % n_y) * steps + at_half * half
                old = lax.dynamic_slice_in_dim(trailing, at, half, axis=0)
                rest = lax.dynamic_update_slice_in_dim(rest, old - total, at, axis=0)

        both = jnp.stack([first, second])
        mine = both[:, :, :quarter]
        theirs = core_swap(both[:, :, quarter:])
        lower = jnp.where(upper, theirs, mine)
        higher = jnp.where(upper, mine, theirs)
        solved = jnp.stack([lower, higher]).reshape(2, 2, comps, half, quarter)
        solved = solved.transpose(0, 3, 2, 1, 4).reshape(steps, comps, 2, quarter)
        return solved, rest

    return body


def solution(mesh):
    placed = (
        P("row", None, None, "col"),
        P(None, None, "col"),
        P(None, "col"),
        P("row", None, "col"),
        P("col", None, "row"),
    )
    return jax.shard_map(
        make_body(mesh.shape["row"], mesh.shape["col"]),
        mesh=mesh,
        in_specs=placed,
        out_specs=(P("row", None, None, "col"), P("col", None, "row")),
        check_vma=False,
    )
```
